32 devices in a mesh: groups: 2 (over x), orb: 16 (over z, y, core).
Axes of the slice: x: 2, y: 2, z: 4, core: 2. Of those that a mesh axis runs over, the one named last changes fastest.
Arguments:
- walkers: bfloat16 [256, 512, 64], P('groups', 'orb'), parts along dimension 0, may hold values from -6 to 6
- cholesky: bfloat16 [2048, 512, 512], P('groups', 'orb'), parts along dimension 0, may hold values from -0.013671875 to 0.013671875
- rotated: bfloat16 [2048, 512, 64], P('groups', 'orb'), parts along dimension 0, may hold values from -0.0068359375 to 0.0068359375
- field_noise: bfloat16 [512, 1024], P('groups'), parts along dimension 0, may hold values from -6 to 6
- sources: int32 [512], P('groups'), parts along dimension 0, may hold values from -1 to 127, as said below
Outputs:
- new_walkers: bfloat16 [512, 512, 64], P('groups', 'orb'), parts along dimension 0
- log_weight: float32 [512], P('groups'), parts along dimension 0
The draws below stay inside these ranges and needn't reach their ends.
There are 2 independent parts, one for each index of `groups`. The reference program is written for one: setup_inputs(seed, part) draws one part's arguments, and reference() takes and returns one part's arrays. A program takes and returns all parts, laid end to end along the dimension named above; each array names one. Nothing has to cross between parts.
Inputs may be any that keep to these rules, and one draw needn't show every extreme that they name: sources[s] names the old walker copied into slot s, or -1 for an empty slot; slot s belongs to owner s // 16, and an owner's live slots come first; exactly 128 slots are live in all; in every draw some owner has all 16 slots live.
All inputs are finite; a program needn't handle non-finite values.
Results may differ from the reference program's by a relative error of at most 0.0085.
Values may be sent and summed in bfloat16 or wider, within the bound.
No kernel may reach another device: no remote copies, remote signals or barrier semaphores. Data moves between devices by JAX's collectives and lax.ppermute only.
A program may use at most 128 MiB of HBM per device.

```python
import jax
import jax.numpy as jnp
from jax import lax

M = 512
NE = 64
NV = 1024
TERMS = 6
WALKERS = 128
CAP = 16
SLOTS = 256
N_ORB = 16


def draw_sources(key, part):
    owners = SLOTS // CAP
    mean_load = WALKERS // owners
    key_order, key_moves, key_pick = jax.random.split(jax.random.fold_in(key, 11), 3)
    order = jax.random.permutation(key_order, owners)
    counts = jnp.full((owners,), mean_load, jnp.int32)
    counts = counts.at[order[0]].set(CAP).at[order[1]].set(2 * mean_load - CAP)
    picks = jax.random.randint(key_moves, (4 * owners, 2), 2, owners)

    def one_move(step, loads):
        giver = order[picks[step, 0]]
        taker = order[picks[step, 1]]
        allowed = ((loads[giver] > 0) & (loads[taker] < CAP) & (giver != taker)).astype(jnp.int32)
        return loads.at[giver].add(-allowed).at[taker].add(allowed)
    counts = lax.fori_loop(0, 4 * owners, one_move, counts)
    chosen = jax.random.randint(key_pick, (SLOTS,), 0, WALKERS)
    slot_rank = jnp.arange(SLOTS, dtype=jnp.int32) % CAP
    owner_of = jnp.arange(SLOTS, dtype=jnp.int32) // CAP
    return jnp.where(slot_rank < counts[owner_of], chosen, -1).astype(jnp.int32)


def block_scale(own_key, shape, cuts, smallest, top_value):
    loudness = 1.0
    for axis_at, parts in cuts:
        heights = jax.random.uniform(jax.random.fold_in(jax.random.fold_in(own_key, 6), axis_at), (parts,), jnp.float32, smallest / len(cuts), top_value / len(cuts))
        loudness = loudness * jnp.repeat(jnp.exp(heights), shape[axis_at] // parts).reshape((-1,) + (1,) * (len(shape) - 1 - axis_at))
    return loudness


def noise(rng, dims, spread, most, shards=(), kind=jnp.bfloat16):
    gain = block_scale(rng, dims, shards, -0.22, 0.18) if shards else 1.0
    drawn = jax.random.normal(rng, dims, jnp.float32) * spread * gain
    return jnp.minimum(jnp.maximum(drawn, -most), most).astype(kind)


def setup_inputs(seed: int = 0, part: int = 0) -> dict:
    seeds = jax.random.split(jax.random.key(seed), 6)
    part_keys = jax.random.split(jax.random.fold_in(seeds[5], part), 6)
    walkers = noise(part_keys[0], (WALKERS, M, NE), 1.0, 6.0, ((1, 16),))
    cholesky = noise(part_keys[1], (NV, M, M), (1.7 / (NV * M) ** 0.5), 0.013671875, ((1, 16),))
    rotated = noise(part_keys[2], (NV, M, NE), (0.2 / (M * NE) ** 0.5), 0.0068359375, ((1, 16),))
    field_noise = noise(part_keys[3], (SLOTS, NV), 1.0, 6.0)
    sources = draw_sources(jax.random.fold_in(jax.random.fold_in(seeds[5], part), 71), part)
    return {"walkers": walkers, "cholesky": cholesky, "rotated": rotated, "field_noise": field_noise, "sources": sources}


def reference(walkers, cholesky, rotated, field_noise, sources):
    count = walkers.shape[0]
    slots = sources.shape[0]
    flat_walk = walkers.reshape(count, M * NE)
    force_bias = lax.dot_general(flat_walk, rotated.reshape(NV, M * NE), (((1,), (1,)), ((), ())), preferred_element_type=jnp.float32)
    is_live = sources >= 0
    source_index = jnp.where(is_live, sources, 0).astype(jnp.int32)
    picked = jnp.where(is_live[:, None], force_bias[source_index], jnp.float32(0.0))
    fields = jnp.where(is_live[:, None], field_noise.astype(jnp.float32) + picked, jnp.float32(0.0))
    log_weight = jnp.sum(fields * picked - 0.5 * picked * picked, axis=1)
    position = jnp.cumsum(is_live.astype(jnp.int32)) - 1
    target = jnp.where(is_live, position, count).astype(jnp.int32)
    compact = jnp.zeros((count,), jnp.int32).at[target].set(jnp.arange(slots, dtype=jnp.int32), mode="drop")
    chosen = fields[compact].astype(jnp.bfloat16)
    starting = walkers[source_index[compact]]
    table = cholesky.reshape(NV, M * M)

    def block_step(block):
        block_fields, block_walk = block
        potential = jnp.dot(block_fields, table, preferred_element_type=jnp.float32).astype(jnp.bfloat16)
        potential = potential.reshape(block_fields.shape[0], M, M).astype(jnp.float32)
        term = block_walk
        total = term.astype(jnp.float32)
        for order in range(1, TERMS):
            product = jnp.einsum("bij,bje->bie", potential, term.astype(jnp.float32))
            term = (product / order).astype(jnp.bfloat16)
            total = total + term.astype(jnp.float32)
        return total.astype(jnp.bfloat16)

    grown = lax.map(block_step, (chosen.reshape(N_ORB, count // N_ORB, NV), starting.reshape(N_ORB, count // N_ORB, M, NE)))
    new_walkers = jnp.zeros((slots, M, NE), jnp.bfloat16).at[compact].set(grown.reshape(count, M, NE))
    return new_walkers, log_weight
```

```python
import functools

import jax
import jax.numpy as jnp
from jax import lax
from jax.experimental import pallas as pl
from jax.experimental.pallas import tpu as pltpu
from jax.sharding import PartitionSpec as P

TERMS = 6
ROWS = 8
LANES = 256
F32 = jnp.float32
BF16 = jnp.bfloat16


def hop(value, mask):
    size = lax.axis_size("orb")
    return lax.ppermute(value, "orb", [(i, i ^ mask) for i in range(size)])


def block_potential(fields, chol):
    swapped = jnp.swapaxes(chol, 0, 1)
    parts = [
        jnp.dot(fields, swapped[i], preferred_element_type=F32) for i in range(ROWS)
    ]
    return jnp.swapaxes(jnp.stack(parts), 0, 1).astype(BF16)


def first_rows_kernel(far, fields, chol, *outs):
    value = block_potential(fields[...], chol[...])
    size = value.shape[0] // far
    for k in range(far):
        outs[k][...] = value[k * size : (k + 1) * size]


def first_rows(fields, cholesky, far):
    slots, vectors = fields.shape
    columns = cholesky.shape[2]
    lanes = min(LANES, columns)
    size = slots // far
    return pl.pallas_call(
        functools.partial(first_rows_kernel, far),
        grid=(columns // lanes,),
        in_specs=[
            pl.BlockSpec((slots, vectors), lambda t: (0, 0)),
            pl.BlockSpec((vectors, ROWS, lanes), lambda t: (0, 0, t)),
        ],
        out_specs=[pl.BlockSpec((size, ROWS, lanes), lambda t: (0, 0, t))] * far,
        out_shape=[jax.ShapeDtypeStruct((size, ROWS, columns), BF16)] * far,
        compiler_params=pltpu.CompilerParams(vmem_limit_bytes=48 << 20),
        cost_estimate=pl.CostEstimate(
            flops=2 * slots * vectors * ROWS * columns,
            bytes_accessed=2 * vectors * ROWS * columns,
            transcendentals=0,
        ),
    )(fields, cholesky)


def other_rows_kernel(near, far, cuts, fields, chol, *outs):
    value = block_potential(fields[...], chol[...])
    each = value.shape[0] // (near * far)
    for g, (low, high) in enumerate(cuts):
        for m in range(near):
            for k in range(far):
                at = (k * near + m) * each
                outs[g * near + m][k] = value[at + low : at + high]


def other_rows(fields, cholesky, near, far, cuts):
    slots, vectors = fields.shape
    rows, columns = cholesky.shape[1:]
    lanes = min(LANES, columns)
    shapes = [(far, high - low, ROWS) for low, high in cuts for _ in range(near)]
    return pl.pallas_call(
        functools.partial(other_rows_kernel, near, far, cuts),
        grid=(rows // ROWS - 1, columns // lanes),
        in_specs=[
            pl.BlockSpec((slots, vectors), lambda r, t: (0, 0)),
            pl.BlockSpec((vectors, ROWS, lanes), lambda r, t: (0, r + 1, t)),
        ],
        out_specs=[
            pl.BlockSpec(shape + (lanes,), lambda r, t: (0, 0, r, t)) for shape in shapes
        ],
        out_shape=[
            jax.ShapeDtypeStruct(shape[:2] + (rows - ROWS, columns), BF16)
            for shape in shapes
        ],
        compiler_params=pltpu.CompilerParams(vmem_limit_bytes=48 << 20),
        cost_estimate=pl.CostEstimate(
            flops=2 * slots * vectors * (rows - ROWS) * columns,
            bytes_accessed=2 * vectors * (rows - ROWS) * columns,
            transcendentals=0,
        ),
    )(fields, cholesky)


def taylor_kernel(near, far, has_rest, me_ref, *refs):
    count = near + (far if has_rest else 0)
    first = refs[:near]
    rest = refs[near:count]
    start = refs[count : count + near]
    outs = refs[count + near : count + 2 * near]
    term = refs[-1]
    me = me_ref[0]
    pair = term.shape[0]
    electrons = term.shape[-1]
    rows = term.shape[2]
    columns = first[0].shape[-1]
    order = [(k, m) for k in range(far) for m in range(near)]

    matrices = []
    totals = []
    for w in range(pair):
        top = jnp.concatenate(
            [first[m][k, w].astype(F32) for k, m in order], axis=0
        ).astype(BF16)
        low = None
        if has_rest:
            low = jnp.concatenate(
                [rest[k][m, w].astype(F32) for k, m in order], axis=0
            ).astype(BF16)
        matrices.append((top, low))
        total_top, total_low = [], []
        for k, m in order:
            value = start[m][k, 0, :, w * electrons : (w + 1) * electrons].astype(F32)
            term[w, me ^ (k * near + m)] = value
            total_top.append(value[:ROWS])
            total_low.append(value[ROWS:])
        totals.append(
            [
                jnp.concatenate(total_top, axis=0),
                jnp.concatenate(total_low, axis=0) if has_rest else None,
            ]
        )
    for step in range(1, TERMS):
        for w in range(pair):
            top, low = matrices[w]
            vector = term[w].reshape(columns, electrons).astype(BF16)
            for part, matrix in enumerate((top, low)):
                if matrix is None:
                    continue
                value = jnp.dot(matrix, vector, preferred_element_type=F32)
                value = (value * F32(1.0 / step)).astype(BF16).astype(F32)
                totals[w][part] = totals[w][part] + value
                if step + 1 < TERMS:
                    size = ROWS if part == 0 else rows - ROWS
                    base = 0 if part == 0 else ROWS
                    for at, (k, m) in enumerate(order):
                        term[w, me ^ (k * near + m), base : base + size] = value[
                            at * size : (at + 1) * size
                        ]
    for at, (k, m) in enumerate(order):
        pieces = []
        for w in range(pair):
            piece = totals[w][0][at * ROWS : (at + 1) * ROWS]
            if has_rest:
                size = rows - ROWS
                tail = totals[w][1][at * size : (at + 1) * size]
                piece = jnp.concatenate([piece, tail], axis=0)
            pieces.append(piece)
        outs[m][k, 0] = jnp.concatenate(pieces, axis=1).astype(BF16)


def taylor(me, first, rest, start, low, high):
    near = len(first)
    far, _, _, columns = first[0].shape
    rows = start[0].shape[2]
    electrons = start[0].shape[3] // 2
    pairs = (high - low) // 2
    has_rest = rest is not None
    in_specs = [
        pl.BlockSpec((far, 2, ROWS, columns), lambda i, me: (0, low // 2 + i, 0, 0))
    ] * near
    args = list(first)
    if has_rest:
        in_specs += [
            pl.BlockSpec((near, 2, rows - ROWS, columns), lambda i, me: (0, i, 0, 0))
        ] * far
        args += list(rest)
    in_specs += [
        pl.BlockSpec(
            (far, 1, rows, 2 * electrons), lambda i, me: (0, low // 2 + i, 0, 0)
        )
    ] * near
    args += list(start)
    return pl.pallas_call(
        functools.partial(taylor_kernel, near, far, has_rest),
        grid_spec=pltpu.PrefetchScalarGridSpec(
            num_scalar_prefetch=1,
            grid=(pairs,),
            in_specs=in_specs,
            out_specs=[
                pl.BlockSpec((far, 1, rows, 2 * electrons), lambda i, me: (0, i, 0, 0))
            ]
            * near,
            scratch_shapes=[pltpu.VMEM((2, near * far, rows, electrons), F32)],
        ),
        out_shape=[jax.ShapeDtypeStruct((far, pairs, rows, 2 * electrons), BF16)] * near,
        compiler_params=pltpu.CompilerParams(vmem_limit_bytes=40 << 20),
        cost_estimate=pl.CostEstimate(
            flops=20 * pairs * columns * columns * electrons,
            bytes_accessed=4 * pairs * columns * columns,
            transcendentals=0,
        ),
    )(me[None], *args)


def far_then_near(blocks, near, far):
    got = [blocks[0]] + [hop(blocks[k], k * near) for k in range(1, far)]
    joined = [jnp.stack([got[k][m] for k in range(far)]) for m in range(near)]
    return [joined[0]] + [hop(joined[m], m) for m in range(1, near)]


def near_then_far(blocks, near, far):
    got = [blocks[0]] + [hop(blocks[m], m) for m in range(1, near)]
    joined = [jnp.stack([got[m][k] for m in range(near)]) for k in range(far)]
    return [joined[0]] + [hop(joined[k], k * near) for k in range(1, far)]


def local(walkers, cholesky, rotated, field_noise, sources):
    count, rows, electrons = walkers.shape
    vectors, _, columns = cholesky.shape
    slots = sources.shape[0]
    devices = lax.axis_size("orb")
    near = 4
    far = devices // near
    each = count // devices
    me = lax.axis_index("orb")
    column = me % near
    chunk = vectors // near

    partial = lax.dot_general(
        walkers.reshape(count, rows * electrons),
        rotated.reshape(vectors, rows * electrons),
        (((1,), (1,)), ((), ())),
        preferred_element_type=F32,
    ).astype(BF16)

    def own(m):
        return lax.dynamic_slice_in_dim(partial, (column ^ m) * chunk, chunk, 1)

    bias = own(0).astype(F32)
    for m in range(1, near):
        bias = bias + hop(own(m), m).astype(F32)
    step = near
    while step < devices:
        bias = bias.astype(BF16)
        bias = bias.astype(F32) + hop(bias, step).astype(F32)
        step *= 2
    bias = bias.astype(BF16)
    parts = jnp.stack([bias] + [hop(bias, m) for m in range(1, near)])
    bias = jnp.concatenate(
        [
            lax.dynamic_index_in_dim(parts, column ^ c, 0, keepdims=False)
            for c in range(near)
        ],
        axis=1,
    )

    is_live = sources >= 0
    position = jnp.cumsum(is_live.astype(jnp.int32)) - 1
    row_index = jnp.arange(count, dtype=jnp.int32)
    wanted = ((row_index // each) ^ me) * each + row_index % each
    place = ((position[None, :] == wanted[:, None]) & is_live[None, :]).astype(BF16)
    named = (sources[:, None] == jnp.arange(count, dtype=jnp.int32)[None, :]).astype(BF16)
    select = jnp.dot(place, named, preferred_element_type=F32).astype(BF16)
    noise = jnp.dot(place, field_noise, preferred_element_type=F32)

    start = jnp.dot(
        select, walkers.reshape(count, rows * electrons), preferred_element_type=F32
    ).astype(BF16)
    start = start.reshape(far, near, each // 2, 2, rows, electrons)
    start = start.transpose(0, 1, 2, 4, 3, 5)
    start = start.reshape(far, near, each // 2, rows, 2 * electrons)
    start = far_then_near([start[k] for k in range(far)], near, far)

    picked = jnp.dot(select, bias, preferred_element_type=F32)
    fields = noise + picked
    weight = jnp.sum(fields * picked - 0.5 * picked * picked, axis=1)
    log_weight = jnp.sum(place.astype(F32) * weight[:, None], axis=0)
    fields = fields.astype(BF16)

    shape = (near, each, ROWS, columns)
    first = [block.reshape(shape) for block in first_rows(fields, cholesky, far)]
    first = far_then_near(first, near, far)
    half = each // 2
    cuts = [(0, half), (half, each)] if rows > ROWS else [(0, each)]
    blocks = other_rows(fields, cholesky, near, far, cuts) if rows > ROWS else None
    results = []
    for g, (low, high) in enumerate(cuts):
        rest = None
        if blocks is not None:
            rest = near_then_far(blocks[g * near : (g + 1) * near], near, far)
        grown = taylor(me, first, rest, start, low, high)
        back = near_then_far(grown, near, far)
        results.append(jnp.stack(back))
    grown = jnp.concatenate(results, axis=2)
    grown = grown.reshape(count // 2, rows, 2, electrons)
    new_walkers = jnp.einsum(
        "xipe,xps->sie", grown, place.reshape(count // 2, 2, slots),
        preferred_element_type=F32,
    ).astype(BF16)
    return (new_walkers, log_weight)


def solution(mesh):
    placed = (
        P("groups", "orb", None),
        P("groups", "orb", None),
        P("groups", "orb", None),
        P("groups", None),
        P("groups"),
    )
    return jax.shard_map(
        local,
        mesh=mesh,
        in_specs=placed,
        out_specs=(P("groups", "orb", None), P("groups")),
        check_vma=False,
    )
```

```python
import functools

import jax
import jax.numpy as jnp
from jax import lax
from jax.experimental import pallas as pl
from jax.experimental.pallas import tpu as pltpu
from jax.sharding import PartitionSpec as P


TERMS = 6
ROWS = 8
LANES = 256
F32 = jnp.float32
BF16 = jnp.bfloat16


def hop(value, mask):
    size = lax.axis_size("orb")
    return lax.ppermute(value, "orb", [(i, i ^ mask) for i in range(size)])


def block_potential(fields, chol):
    swapped = jnp.swapaxes(chol, 0, 1)
    parts = [
        jnp.dot(fields, swapped[i], preferred_element_type=F32) for i in range(ROWS)
    ]
    return jnp.swapaxes(jnp.stack(parts), 0, 1).astype(BF16)


def some_rows_kernel(far, fields, chol, *outs):
    value = block_potential(fields[...], chol[...])
    size = value.shape[0] // far
    for k in range(far):
        outs[k][...] = value[k * size : (k + 1) * size]


def some_rows(fields, cholesky, far, block):
    slots, vectors = fields.shape
    columns = cholesky.shape[2]
    lanes = min(LANES, columns)
    size = slots // far
    return pl.pallas_call(
        functools.partial(some_rows_kernel, far),
        grid=(columns // lanes,),
        in_specs=[
            pl.BlockSpec((slots, vectors), lambda t: (0, 0)),
            pl.BlockSpec((vectors, ROWS, lanes), lambda t: (0, block, t)),
        ],
        out_specs=[pl.BlockSpec((size, ROWS, lanes), lambda t: (0, 0, t))] * far,
        out_shape=[jax.ShapeDtypeStruct((size, ROWS, columns), BF16)] * far,
        compiler_params=pltpu.CompilerParams(vmem_limit_bytes=48 << 20),
        cost_estimate=pl.CostEstimate(
            flops=2 * slots * vectors * ROWS * columns,
            bytes_accessed=2 * vectors * ROWS * columns,
            transcendentals=0,
        ),
    )(fields, cholesky)


def other_rows_kernel(near, far, cuts, fields, chol, *outs):
    value = block_potential(fields[...], chol[...])
    each = value.shape[0] // (near * far)
    for g, (low, high) in enumerate(cuts):
        for m in range(near):
            for k in range(far):
                at = (k * near + m) * each
                outs[g * near + m][k] = value[at + low : at + high]


def other_rows(fields, cholesky, near, far, cuts, done):
    slots, vectors = fields.shape
    rows, columns = cholesky.shape[1:]
    lanes = min(LANES, columns)
    shapes = [(far, high - low, ROWS) for low, high in cuts for _ in range(near)]
    return pl.pallas_call(
        functools.partial(other_rows_kernel, near, far, cuts),
        grid=(rows // ROWS - done, columns // lanes),
        in_specs=[
            pl.BlockSpec((slots, vectors), lambda r, t: (0, 0)),
            pl.BlockSpec((vectors, ROWS, lanes), lambda r, t: (0, r + done, t)),
        ],
        out_specs=[
            pl.BlockSpec(shape + (lanes,), lambda r, t: (0, 0, r, t)) for shape in shapes
        ],
        out_shape=[
            jax.ShapeDtypeStruct(shape[:2] + (rows - done * ROWS, columns), BF16)
            for shape in shapes
        ],
        compiler_params=pltpu.CompilerParams(vmem_limit_bytes=48 << 20),
        cost_estimate=pl.CostEstimate(
            flops=2 * slots * vectors * (rows - done * ROWS) * columns,
            bytes_accessed=2 * vectors * (rows - done * ROWS) * columns,
            transcendentals=0,
        ),
    )(fields, cholesky)


def taylor_kernel(near, far, tops, has_rest, me_ref, *refs):
    at = tops * near
    first = [refs[i * near : (i + 1) * near] for i in range(tops)]
    rest = refs[at : at + far] if has_rest else None
    at += far if has_rest else 0
    start = refs[at : at + near]
    outs = refs[at + near : at + 2 * near]
    terms = refs[at + 2 * near :]
    me = me_ref[0]
    group = len(terms)
    rows, electrons = terms[0].shape[1:]
    columns = first[0][0].shape[-1]
    order = [(k, m) for k in range(far) for m in range(near)]
    spans = [(i * ROWS, (i + 1) * ROWS) for i in range(tops)]
    if has_rest:
        spans.append((tops * ROWS, rows))

    def joined(pieces):
        wide = [piece.astype(F32) for piece in pieces]
        return jnp.concatenate(wide, axis=0).astype(BF16)

    matrices = []
    totals = []
    for w in range(group):
        blocks = [joined([part[m][k, w] for k, m in order]) for part in first]
        if has_rest:
            blocks.append(joined([rest[k][m, w] for k, m in order]))
        matrices.append(blocks)
        values = []
        for k, m in order:
            side = (w % 2) * electrons
            value = start[m][k, w // 2, :, side : side + electrons].astype(F32)
            terms[w][me ^ (k * near + m)] = value
            values.append(value)
        totals.append(
            [
                jnp.concatenate([value[low:high] for value in values], axis=0)
                for low, high in spans
            ]
        )
    for step in range(1, TERMS):
        for w in range(group):
            vector = terms[w][...].reshape(columns, electrons).astype(BF16)
            for part, (low, high) in enumerate(spans):
                size = high - low
                value = jnp.dot(matrices[w][part], vector, preferred_element_type=F32)
                value = (value * F32(1.0 / step)).astype(BF16).astype(F32)
                totals[w][part] = totals[w][part] + value
                if step + 1 < TERMS:
                    for i, (k, m) in enumerate(order):
                        terms[w][me ^ (k * near + m), low:high] = value[
                            i * size : (i + 1) * size
                        ]
    for i, (k, m) in enumerate(order):
        pieces = []
        for w in range(group):
            piece = [
                totals[w][part][i * (high - low) : (i + 1) * (high - low)]
                for part, (low, high) in enumerate(spans)
            ]
            pieces.append(jnp.concatenate(piece, axis=0))
        for w in range(0, group, 2):
            outs[m][k, w // 2] = jnp.concatenate(pieces[w : w + 2], axis=1).astype(BF16)


def taylor(me, first, rest, start, low, high):
    near = len(start)
    far = start[0].shape[0]
    columns = first[0][0].shape[3]
    rows = start[0].shape[2]
    electrons = start[0].shape[3] // 2
    pairs = (high - low) // 2
    group = high - low if high - low <= 4 and low % (high - low) == 0 else 2
    half = group // 2
    in_specs = [
        pl.BlockSpec(
            (far, group, ROWS, columns), lambda i, me: (0, low // group + i, 0, 0)
        )
    ] * (near * len(first))
    args = [block for part in first for block in part]
    if rest is not None:
        in_specs += [
            pl.BlockSpec((near, group) + rest[0].shape[2:], lambda i, me: (0, i, 0, 0))
        ] * far
        args += list(rest)
    in_specs += [
        pl.BlockSpec(
            (far, half, rows, 2 * electrons), lambda i, me: (0, low // group + i, 0, 0)
        )
    ] * near
    args += list(start)
    return pl.pallas_call(
        functools.partial(taylor_kernel, near, far, len(first), rest is not None),
        grid_spec=pltpu.PrefetchScalarGridSpec(
            num_scalar_prefetch=1,
            grid=((high - low) // group,),
            in_specs=in_specs,
            out_specs=[
                pl.BlockSpec((far, half, rows, 2 * electrons), lambda i, me: (0, i, 0, 0))
            ]
            * near,
            scratch_shapes=[pltpu.VMEM((near * far, rows, electrons), F32)] * group,
        ),
        out_shape=[jax.ShapeDtypeStruct((far, pairs, rows, 2 * electrons), BF16)] * near,
        compiler_params=pltpu.CompilerParams(vmem_limit_bytes=40 << 20),
        cost_estimate=pl.CostEstimate(
            flops=20 * pairs * columns * columns * electrons,
            bytes_accessed=4 * pairs * columns * columns,
            transcendentals=0,
        ),
    )(me[None], *args)


def far_hops(blocks, near):
    return [blocks[0]] + [hop(blocks[k], k * near) for k in range(1, len(blocks))]


def near_hops(blocks):
    return [blocks[0]] + [hop(blocks[m], m) for m in range(1, len(blocks))]


def far_then_near(blocks, near, far):
    got = far_hops(blocks, near)
    joined = [jnp.stack([got[k][m] for k in range(far)]) for m in range(near)]
    return near_hops(joined)


def near_then_far(blocks, near, far):
    got = near_hops(blocks)
    joined = [jnp.stack([got[m][k] for m in range(near)]) for k in range(far)]
    return far_hops(joined, near)


def local(walkers, cholesky, rotated, field_noise, sources):
    count, rows, electrons = walkers.shape
    vectors, _, columns = cholesky.shape
    slots = sources.shape[0]
    devices = lax.axis_size("orb")
    near = 4
    far = devices // near
    each = count // devices
    me = lax.axis_index("orb")
    column = me % near
    chunk = vectors // near

    partial = lax.dot_general(
        walkers.reshape(count, rows * electrons),
        rotated.reshape(vectors, rows * electrons),
        (((1,), (1,)), ((), ())),
        preferred_element_type=F32,
    ).astype(BF16)

    def own(m):
        return lax.dynamic_slice_in_dim(partial, (column ^ m) * chunk, chunk, 1)

    bias = sum(part.astype(F32) for part in near_hops([own(m) for m in range(near)]))
    shift = near
    while shift < devices:
        bias = bias.astype(BF16)
        bias = bias.astype(F32) + hop(bias, shift).astype(F32)
        shift *= 2
    parts = jnp.stack(near_hops([bias.astype(BF16)] * near))
    bias = jnp.concatenate(
        [
            lax.dynamic_index_in_dim(parts, column ^ c, 0, keepdims=False)
            for c in range(near)
        ],
        axis=1,
    )

    is_live = sources >= 0
    position = jnp.cumsum(is_live.astype(jnp.int32)) - 1
    row_index = jnp.arange(count, dtype=jnp.int32)
    wanted = ((row_index // each) ^ me) * each + row_index % each
    place = ((position[None, :] == wanted[:, None]) & is_live[None, :]).astype(BF16)
    named = (sources[:, None] == jnp.arange(count, dtype=jnp.int32)[None, :]).astype(BF16)
    select = jnp.dot(place, named, preferred_element_type=F32).astype(BF16)
    noise = jnp.dot(place, field_noise, preferred_element_type=F32)

    start = jnp.dot(
        select, walkers.reshape(count, rows * electrons), preferred_element_type=F32
    ).astype(BF16)
    start = start.reshape(far, near, each // 2, 2, rows, electrons)
    start = start.transpose(0, 1, 2, 4, 3, 5)
    start = start.reshape(far, near, each // 2, rows, 2 * electrons)
    start = far_then_near([start[k] for k in range(far)], near, far)

    picked = jnp.dot(select, bias, preferred_element_type=F32)
    fields = noise + picked
    weight = jnp.sum(fields * picked - 0.5 * picked * picked, axis=1)
    log_weight = jnp.sum(place.astype(F32) * weight[:, None], axis=0)
    fields = fields.astype(BF16)

    shape = (near, each, ROWS, columns)
    tops = min(2, rows // ROWS)
    first = []
    for i in range(tops):
        part = some_rows(fields, cholesky, far, i)
        part = [block.reshape(shape) for block in part]
        first.append(far_then_near(part, near, far))
    blocks = None
    cuts = [(0, each)]
    if rows > tops * ROWS:
        cuts = [(0, each // 2), (each // 2, each)]
        blocks = other_rows(fields, cholesky, near, far, cuts, tops)
    results = []
    for g, (low, high) in enumerate(cuts):
        rest = None
        if blocks is not None:
            mine = blocks[g * near : (g + 1) * near]
            rest = near_then_far(mine, near, far)
        grown = taylor(me, first, rest, start, low, high)
        back = near_then_far(grown, near, far)
        results.append(jnp.stack(back))
    grown = jnp.concatenate(results, axis=2)
    grown = grown.reshape(count // 2, rows, 2, electrons)
    new_walkers = jnp.einsum(
        "xipe,xps->sie", grown, place.reshape(count // 2, 2, slots),
        preferred_element_type=F32,
    ).astype(BF16)
    return (new_walkers, log_weight)


def solution(mesh):
    placed = (
        P("groups", "orb", None),
        P("groups", "orb", None),
        P("groups", "orb", None),
        P("groups", None),
        P("groups"),
    )


    return jax.shard_map(
        local,
        mesh=mesh,
        in_specs=placed,
        out_specs=(P("groups", "orb", None), P("groups")),
        check_vma=False,
    )
```

```python
import functools

import jax
import jax.numpy as jnp
from jax import lax
from jax.experimental import pallas as pl
from jax.experimental.pallas import tpu as pltpu
from jax.sharding import PartitionSpec as P


TERMS = 6
ROWS = 8
SPLIT = 1
LANES = 256
F32 = jnp.float32
BF16 = jnp.bfloat16


def CUTS(each):
    return [(0, each // 2), (each // 2, each)]


def hop(value, mask):
    size = lax.axis_size("orb")
    return lax.ppermute(value, "orb", [(i, i ^ mask) for i in range(size)])


def block_potential(fields, chol):
    swapped = jnp.swapaxes(chol, 0, 1)
    parts = [
        jnp.dot(fields, swapped[i], preferred_element_type=F32) for i in range(ROWS)
    ]
    return jnp.swapaxes(jnp.stack(parts), 0, 1).astype(BF16)


def some_rows_kernel(far, fields, chol, *outs):
    value = block_potential(fields[...], chol[...])
    size = value.shape[0] // far
    for k in range(far):
        outs[k][...] = value[k * size : (k + 1) * size]


def some_rows(fields, cholesky, far, block, cut, cuts):
    slots, vectors = fields.shape
    columns = cholesky.shape[2] // cuts
    lanes = min(LANES, columns)
    size = slots // far
    skip = cut * (columns // lanes)
    return pl.pallas_call(
        functools.partial(some_rows_kernel, far),
        grid=(columns // lanes,),
        in_specs=[
            pl.BlockSpec((slots, vectors), lambda t: (0, 0)),
            pl.BlockSpec((vectors, ROWS, lanes), lambda t: (0, block, skip + t)),
        ],
        out_specs=[pl.BlockSpec((size, ROWS, lanes), lambda t: (0, 0, t))] * far,
        out_shape=[jax.ShapeDtypeStruct((size, ROWS, columns), BF16)] * far,
        compiler_params=pltpu.CompilerParams(vmem_limit_bytes=32 << 20),
        cost_estimate=pl.CostEstimate(
            flops=2 * slots * vectors * ROWS * columns,
            bytes_accessed=2 * vectors * ROWS * columns,
            transcendentals=0,
        ),
    )(fields, cholesky)


def swap_kernel(chol, out):
    out[...] = jnp.swapaxes(chol[...], 0, 1)


def swapped_rows(cholesky, cut, cuts):
    vectors, _, columns = cholesky.shape
    columns //= cuts
    lanes = min(LANES // 2, columns)
    skip = cut * (columns // lanes)
    return pl.pallas_call(
        swap_kernel,
        grid=(columns // lanes,),
        in_specs=[pl.BlockSpec((vectors, ROWS, lanes), lambda t: (0, 0, skip + t))],
        out_specs=pl.BlockSpec((ROWS, vectors, lanes), lambda t: (0, 0, t)),
        out_shape=jax.ShapeDtypeStruct((ROWS, vectors, columns), BF16),
        compiler_params=pltpu.CompilerParams(vmem_limit_bytes=24 << 20),
        cost_estimate=pl.CostEstimate(
            flops=0, bytes_accessed=2 * vectors * ROWS * columns, transcendentals=0
        ),
    )(cholesky)


def swapped_kernel(far, parts, fields, *refs):
    outs = refs[parts:]
    size = fields.shape[0] // far
    for p in range(parts):
        columns = refs[p].shape[2]
        value = [
            jnp.dot(fields[...], refs[p][i], preferred_element_type=F32)
            for i in range(ROWS)
        ]
        value = jnp.swapaxes(jnp.stack(value), 0, 1).astype(BF16)
        for k in range(far):
            outs[k][:, :, p * columns : (p + 1) * columns] = value[
                k * size : (k + 1) * size
            ]


def first_rows(fields, blocks, far):
    slots = fields.shape[0]
    columns = sum(block.shape[2] for block in blocks)
    space = pl.BlockSpec(memory_space=pltpu.VMEM)
    return pl.pallas_call(
        functools.partial(swapped_kernel, far, len(blocks)),
        in_specs=[space] * (1 + len(blocks)),
        out_specs=[space] * far,
        out_shape=[jax.ShapeDtypeStruct((slots // far, ROWS, columns), BF16)] * far,
        compiler_params=pltpu.CompilerParams(vmem_limit_bytes=32 << 20),
        cost_estimate=pl.CostEstimate(
            flops=2 * slots * blocks[0].shape[1] * ROWS * columns,
            bytes_accessed=1 << 20,
            transcendentals=0,
        ),
    )(fields, *blocks)


def other_rows_kernel(near, far, cuts, fields, chol, *outs):
    value = block_potential(fields[...], chol[...])
    each = value.shape[0] // (near * far)
    for g, (low, high) in enumerate(cuts):
        for m in range(near):
            for k in range(far):
                at = (k * near + m) * each
                outs[g * near + m][k] = value[at + low : at + high]


def other_rows(fields, cholesky, near, far, cuts, done):
    slots, vectors = fields.shape
    rows, columns = cholesky.shape[1:]
    lanes = min(LANES, columns)
    shapes = [(far, high - low, ROWS) for low, high in cuts for _ in range(near)]
    return pl.pallas_call(
        functools.partial(other_rows_kernel, near, far, cuts),
        grid=(rows // ROWS - done, columns // lanes),
        in_specs=[
            pl.BlockSpec((slots, vectors), lambda r, t: (0, 0)),
            pl.BlockSpec((vectors, ROWS, lanes), lambda r, t: (0, r + done, t)),
        ],
        out_specs=[
            pl.BlockSpec(shape + (lanes,), lambda r, t: (0, 0, r, t)) for shape in shapes
        ],
        out_shape=[
            jax.ShapeDtypeStruct(shape[:2] + (rows - done * ROWS, columns), BF16)
            for shape in shapes
        ],
        compiler_params=pltpu.CompilerParams(vmem_limit_bytes=32 << 20),
        cost_estimate=pl.CostEstimate(
            flops=2 * slots * vectors * (rows - done * ROWS) * columns,
            bytes_accessed=2 * vectors * (rows - done * ROWS) * columns,
            transcendentals=0,
        ),
    )(fields, cholesky)


def taylor_kernel(near, far, pieces, has_rest, walker, me_ref, *refs):
    tops = len(pieces)
    first = []
    at = 0
    for count in pieces:
        first.append([refs[at + i * near : at + (i + 1) * near] for i in range(count)])
        at += count * near
    rest = refs[at : at + far] if has_rest else None
    at += far if has_rest else 0
    start = refs[at : at + near]
    outs = refs[at + near : at + 2 * near]
    terms = refs[at + 2 * near :]
    me = me_ref[0]
    group = len(terms)
    rows, electrons = terms[0].shape[1:]
    columns = near * far * rows
    order = [(k, m) for k in range(far) for m in range(near)]
    spans = [(i * ROWS, (i + 1) * ROWS) for i in range(tops)]
    if has_rest:
        spans.append((tops * ROWS, rows))

    def joined(pieces):
        wide = [piece.astype(F32) for piece in pieces]
        return jnp.concatenate(wide, axis=0).astype(BF16)

    opened = {
        (k, m): jnp.swapaxes(start[m][k].astype(F32), 0, 1) for k, m in order
    }
    matrices = []
    totals = []
    for w in range(group):
        blocks = []
        for part in first:
            wide = [joined([cut[m][k, w] for k, m in order]) for cut in part]
            blocks.append(jnp.concatenate(wide, axis=1))
        if has_rest:
            blocks.append(joined([rest[k][m, w] for k, m in order]))
        matrices.append(blocks)
        values = []
        for k, m in order:
            pairs = opened[k, m][walker + w]
            block = me ^ (k * near + m)
            for side in range(2):
                terms[w][block, pl.ds(side, rows // 2, stride=2), :] = pairs[
                    :, side * electrons : (side + 1) * electrons
                ]
            values.append(terms[w][block])
        totals.append(
            [
                jnp.concatenate([value[low:high] for value in values], axis=0)
                for low, high in spans
            ]
        )
    for step in range(1, TERMS):
        for w in range(group):
            vector = terms[w][...].reshape(columns, electrons).astype(BF16)
            for part, (low, high) in enumerate(spans):
                size = high - low
                value = jnp.dot(matrices[w][part], vector, preferred_element_type=F32)
                value = (value * F32(1.0 / step)).astype(BF16).astype(F32)
                totals[w][part] = totals[w][part] + value
                if step + 1 < TERMS:
                    for i, (k, m) in enumerate(order):
                        terms[w][me ^ (k * near + m), low:high] = value[
                            i * size : (i + 1) * size
                        ]
    for i, (k, m) in enumerate(order):
        whole = []
        for w in range(group):
            piece = [
                totals[w][part][i * (high - low) : (i + 1) * (high - low)]
                for part, (low, high) in enumerate(spans)
            ]
            whole.append(jnp.concatenate(piece, axis=0))
        for w in range(0, group, 2):
            outs[m][k, w // 2] = jnp.concatenate(whole[w : w + 2], axis=1).astype(BF16)


def taylor(me, first, rest, start, low, high):
    near = len(start)
    far = start[0].shape[0]
    rows = 2 * start[0].shape[1]
    columns = near * far * rows
    electrons = start[0].shape[3] // 2
    pairs = (high - low) // 2
    group = high - low if high - low <= 4 and low % (high - low) == 0 else 2
    half = group // 2
    args = [block for part in first for cut in part for block in cut]
    in_specs = [
        pl.BlockSpec(
            (far, group, ROWS, block.shape[3]),
            lambda i, me: (0, low // group + i, 0, 0),
        )
        for block in args
    ]
    if rest is not None:
        in_specs += [
            pl.BlockSpec((near, group) + rest[0].shape[2:], lambda i, me: (0, i, 0, 0))
        ] * far
        args += list(rest)
    in_specs += [
        pl.BlockSpec(
            start[0].shape, lambda i, me: (0, 0, 0, 0)
        )
    ] * near
    args += list(start)
    return pl.pallas_call(
        functools.partial(
            taylor_kernel,
            near,
            far,
            [len(part) for part in first],
            rest is not None,
            low,
        ),
        grid_spec=pltpu.PrefetchScalarGridSpec(
            num_scalar_prefetch=1,
            grid=((high - low) // group,),
            in_specs=in_specs,
            out_specs=[
                pl.BlockSpec((far, half, rows, 2 * electrons), lambda i, me: (0, i, 0, 0))
            ]
            * near,
            scratch_shapes=[pltpu.VMEM((near * far, rows, electrons), F32)] * group,
        ),
        out_shape=[jax.ShapeDtypeStruct((far, pairs, rows, 2 * electrons), BF16)] * near,
        compiler_params=pltpu.CompilerParams(vmem_limit_bytes=32 << 20),
        cost_estimate=pl.CostEstimate(
            flops=20 * pairs * columns * columns * electrons,
            bytes_accessed=4 * pairs * columns * columns,
            transcendentals=0,
        ),
    )(me[None], *args)


def far_hops(blocks, near):
    got = list(blocks)
    for k in sorted(range(1, len(blocks)), key=lambda k: -k.bit_length()):
        got[k] = hop(blocks[k], k * near)
    return got


def near_hops(blocks):
    return [blocks[0]] + [hop(blocks[m], m) for m in range(1, len(blocks))]


def far_then_near(blocks, near, far):
    got = far_hops(blocks, near)
    joined = [jnp.stack([got[k][m] for k in range(far)]) for m in range(near)]
    return near_hops(joined)


def near_then_far(blocks, near, far):
    got = near_hops(blocks)
    joined = [jnp.stack([got[m][k] for m in range(near)]) for k in range(far)]
    return far_hops(joined, near)


def local(walkers, cholesky, rotated, field_noise, sources):
    count, rows, electrons = walkers.shape
    vectors, _, columns = cholesky.shape
    slots = sources.shape[0]
    devices = lax.axis_size("orb")
    near = 4
    far = devices // near
    each = count // devices
    me = lax.axis_index("orb")
    column = me % near
    chunk = vectors // near

    partial = lax.dot_general(
        walkers.reshape(count, rows * electrons),
        rotated.reshape(vectors, rows * electrons),
        (((1,), (1,)), ((), ())),
        preferred_element_type=F32,
    ).astype(BF16)

    def piece(c):
        return lax.dynamic_slice_in_dim(partial, c * chunk, chunk, 1)

    left = near // 2
    side = column % 2
    keep = [piece(2 * c + side) for c in range(left)]
    give = [piece(2 * c + 1 - side) for c in range(left)]
    shift = 1
    while True:
        got = hop(jnp.stack(give), shift)
        total = [mine.astype(F32) + got[c].astype(F32) for c, mine in enumerate(keep)]
        if left == 1:
            break
        shift *= 2
        left //= 2
        side = (column // shift) % 2
        total = jnp.stack(total).astype(BF16)
        keep = [
            lax.dynamic_index_in_dim(total, 2 * c + side, 0, keepdims=False)
            for c in range(left)
        ]
        give = [
            lax.dynamic_index_in_dim(total, 2 * c + 1 - side, 0, keepdims=False)
            for c in range(left)
        ]
    bias = total[0]
    shift = near
    while shift < devices:
        bias = bias.astype(BF16)
        bias = bias.astype(F32) + hop(bias, shift).astype(F32)
        shift *= 2
    parts = jnp.stack(near_hops([bias.astype(BF16)] * near))
    bias = jnp.concatenate(
        [
            lax.dynamic_index_in_dim(parts, column ^ c, 0, keepdims=False)
            for c in range(near)
        ],
        axis=1,
    )

    is_live = sources >= 0
    position = jnp.cumsum(is_live.astype(jnp.int32)) - 1
    row_index = jnp.arange(count, dtype=jnp.int32)
    wanted = ((row_index // each) ^ me) * each + row_index % each
    place = ((position[None, :] == wanted[:, None]) & is_live[None, :]).astype(BF16)
    named = (sources[:, None] == jnp.arange(count, dtype=jnp.int32)[None, :]).astype(BF16)
    select = jnp.dot(place, named, preferred_element_type=F32).astype(BF16)
    noise = jnp.dot(place, field_noise, preferred_element_type=F32)

    start = jnp.einsum(
        "sw,wpl->psl",
        select,
        walkers.reshape(count, rows // 2, 2 * electrons),
        preferred_element_type=F32,
    ).astype(BF16)
    start = start.reshape(rows // 2, far, near * each, 2 * electrons)
    start = far_hops([start[:, k] for k in range(far)], near)
    start = near_hops(
        [
            jnp.stack([part[:, m * each : (m + 1) * each] for part in start])
            for m in range(near)
        ],
    )

    picked = jnp.dot(select, bias, preferred_element_type=F32)
    fields = noise + picked
    weight = jnp.sum(fields * picked - 0.5 * picked * picked, axis=1)
    log_weight = jnp.sum(place.astype(F32) * weight[:, None], axis=0)
    fields = fields.astype(BF16)

    ahead = []
    for cut in range(2):
        ahead.append(swapped_rows(cholesky, cut, 2))
    tops = min(2, rows // ROWS)
    first = []
    for i in range(tops):
        parts = SPLIT if i == 0 and columns >= 2 * LANES else 1
        first.append([])
        for cut in range(parts):
            if i == 0:
                part = first_rows(fields, ahead, far)
            else:
                part = some_rows(fields, cholesky, far, i, cut, parts)
            part = [
                block.reshape(near, each, ROWS, columns // parts) for block in part
            ]
            first[i].append(far_then_near(part, near, far))
    blocks = None
    cuts = [(0, each)]
    if rows > tops * ROWS:
        cuts = CUTS(each)
        blocks = other_rows(fields, cholesky, near, far, cuts, tops)
    results = []
    for g, (low, high) in enumerate(cuts):
        rest = None
        if blocks is not None:
            mine = blocks[g * near : (g + 1) * near]
            rest = near_then_far(mine, near, far)
        grown = taylor(me, first, rest, start, low, high)
        back = near_then_far(grown, near, far)
        results.append(jnp.stack(back))
    grown = jnp.concatenate(results, axis=2)
    grown = grown.reshape(count // 2, rows, 2, electrons)
    new_walkers = jnp.einsum(
        "xipe,xps->sie", grown, place.reshape(count // 2, 2, slots),
        preferred_element_type=F32,
    ).astype(BF16)
    return (new_walkers, log_weight)


def solution(mesh):
    placed = (
        P("groups", "orb", None),
        P("groups", "orb", None),
        P("groups", "orb", None),
        P("groups", None),
        P("groups"),
    )


    return jax.shard_map(
        local,
        mesh=mesh,
        in_specs=placed,
        out_specs=(P("groups", "orb", None), P("groups")),
        check_vma=False,
    )
```
